32 devices in a mesh: ex: 8 (over z, y), par: 4 (over x, core).
Axes of the slice: x: 2, y: 2, z: 4, core: 2. Of those that a mesh axis runs over, the one named last changes fastest.
Arguments:
- gradients: bfloat16 [512, 16384], P('ex', 'par'), may hold values from -6 to 6
- inverse_gram: bfloat16 [16384, 16384], P('par', 'ex'), may hold values from -1 to 3
- hash_words: int32 [4], replicated, may hold values from 1 to 2147483646
Outputs:
- scores: float32 [512, 512], P('par', 'ex')
The draws below stay inside these ranges and needn't reach their ends.
All inputs are finite; a program needn't handle non-finite values.
Results may differ from the reference program's by a relative error of at most 0.0003.
Values may be sent and summed in bfloat16 or wider, within the bound.
A program may use at most 64 MiB of HBM per device.

```python
import math
import jax
import jax.numpy as jnp
from jax import lax

FEATURES = 16384
EXAMPLES = 512
PARAMS = 16384


def draw_inverse_gram(key, part):
    off_key, diag_key = jax.random.split(jax.random.fold_in(key, 11))
    spread = 0.5 / math.sqrt(FEATURES)
    off_part = jax.random.truncated_normal(off_key, -4.0, 4.0, (FEATURES, FEATURES), jnp.float32) * spread
    diagonal = jax.random.uniform(diag_key, (FEATURES,), jnp.float32, 0.5, 2.0)
    diag_ids = jnp.arange(FEATURES)
    return off_part.at[diag_ids, diag_ids].add(diagonal).astype(jnp.bfloat16)


def touch_ends(array, key, smallest, high):
    index_at = [jax.random.randint(jax.random.fold_in(key, axis), (), 0, length) for axis, length in enumerate(array.shape)]
    longest = array.shape.index(max(array.shape))
    next_to = index_at[:longest] + [(index_at[longest] + 1) % array.shape[longest]] + index_at[longest + 1:]
    return array.at[tuple(index_at)].set(smallest).at[tuple(next_to)].set(high)


def shard_levels(own_key, shape, pieces, low, largest):
    loudness = 1.0
    for dim, parts in pieces:
        draws = jax.random.uniform(jax.random.fold_in(jax.random.fold_in(own_key, 6), dim), (parts,), jnp.float32, low / len(pieces), largest / len(pieces))
        loudness = loudness * jnp.repeat(jnp.exp(draws), shape[dim] // parts).reshape((-1,) + (1,) * (len(shape) - 1 - dim))
    return loudness


def scatter_about(own_key, shape, deviation, most, cuts=(), held_as=jnp.bfloat16):
    entries = deviation * jax.random.normal(own_key, shape, jnp.float32)
    if cuts:
        entries = entries * shard_levels(own_key, shape, cuts, -0.22, 0.18)
    return jnp.clip(entries, -most, most).astype(held_as)


def setup_inputs(seed: int = 0) -> dict:
    key_list = jax.random.split(jax.random.key(seed), 4)
    gradients = scatter_about(key_list[0], (EXAMPLES, PARAMS), 1.0, 6.0, ((0, 8), (1, 4)))
    inverse_gram = draw_inverse_gram(jax.random.fold_in(key_list[3], 71), 0)
    hash_words = touch_ends(jax.random.randint(key_list[2], (4,), 1, 2147483647), jax.random.fold_in(key_list[2], 1), 1, 2147483646).astype(jnp.int32)
    return {"gradients": gradients, "inverse_gram": inverse_gram, "hash_words": hash_words}


def shifted(values, amount):
    return lax.shift_right_logical(values, jnp.full(values.shape, amount, jnp.int32))


def hash_table(hash_words, row_start, row_count, col_start, col_count):
    row_ids = lax.broadcasted_iota(jnp.int32, (row_count, col_count), 0) + row_start
    col_ids = lax.broadcasted_iota(jnp.int32, (row_count, col_count), 1) + col_start
    mixed = row_ids * FEATURES + col_ids
    mixed = mixed * (hash_words[0] | 1) + hash_words[1]
    mixed = mixed ^ shifted(mixed, 15)
    mixed = mixed * (hash_words[2] | 1)
    mixed = mixed ^ shifted(mixed, 13)
    mixed = mixed * (hash_words[3] | 1)
    mixed = mixed ^ shifted(mixed, 16)
    top_bit = shifted(mixed, 31)
    return ((1 - 2 * top_bit).astype(jnp.float32) * (FEATURES ** -0.5)).astype(jnp.bfloat16)


def reference(gradients, inverse_gram, hash_words):
    param_count = gradients.shape[1]
    col_width = min(1024, FEATURES)
    block_count = FEATURES // col_width

    def column_block(col_start):
        sign_table = hash_table(hash_words, 0, param_count, col_start, col_width)
        return jnp.dot(gradients, sign_table, preferred_element_type=jnp.float32)

    col_starts = jnp.arange(block_count, dtype=jnp.int32) * col_width
    blocks = lax.map(column_block, col_starts)
    features = jnp.transpose(blocks, (1, 0, 2)).reshape(gradients.shape[0], FEATURES).astype(jnp.bfloat16)
    conditioned = jnp.dot(features, inverse_gram, preferred_element_type=jnp.float32).astype(jnp.bfloat16)
    pairs = jnp.dot(conditioned, features.T, preferred_element_type=jnp.float32)
    return pairs * (FEATURES ** -0.5)
```

```python
import functools

import jax
import jax.numpy as jnp
from jax import lax
from jax.experimental import pallas as pl
from jax.experimental.pallas import tpu as pltpu
from jax.sharding import PartitionSpec as P

FEATURES = 16384


def shifted(values, amount):
    return lax.shift_right_logical(values, jnp.full(values.shape, amount, jnp.int32))


def hash_kernel(tile, words_ref, start_ref, cols_ref, grads_ref, out_ref):
    step = pl.program_id(0)
    depth = grads_ref.shape[1]
    m0 = words_ref[0] | 1
    m2 = words_ref[2] | 1
    m3 = words_ref[3] | 1
    row_base = (start_ref[0] + step * depth) * FEATURES * m0 + words_ref[1]
    rows = lax.broadcasted_iota(jnp.int32, (depth, tile), 0) * (m0 * FEATURES)
    grads = grads_ref[...]
    for first in range(0, out_ref.shape[1], tile):
        mixed = rows + (cols_ref[:, first:first + tile] * m0 + row_base)
        mixed = (mixed ^ shifted(mixed, 15)) * m2
        mixed = (mixed ^ shifted(mixed, 13)) * m3
        signs = jnp.where(mixed < 0, -1.0, 1.0).astype(jnp.bfloat16)
        part = jnp.dot(grads, signs, preferred_element_type=jnp.float32)

        @pl.when(step == 0)
        def _():
            out_ref[:, first:first + tile] = part

        @pl.when(step > 0)
        def _():
            out_ref[:, first:first + tile] += part


def project(words, start, cols, grads):
    rows, amount = grads.shape
    width = cols.shape[1]
    depth = min(512, amount)
    tile = min(512, width)
    return pl.pallas_call(
        functools.partial(hash_kernel, tile),
        grid=(amount // depth,),
        in_specs=[
            pl.BlockSpec(memory_space=pltpu.SMEM),
            pl.BlockSpec(memory_space=pltpu.SMEM),
            pl.BlockSpec((1, width), lambda k: (0, 0)),
            pl.BlockSpec((rows, depth), lambda k: (0, k)),
        ],
        out_specs=pl.BlockSpec((rows, width), lambda k: (0, 0)),
        out_shape=jax.ShapeDtypeStruct((rows, width), jnp.float32),
        compiler_params=pltpu.CompilerParams(
            dimension_semantics=("arbitrary",), vmem_limit_bytes=48 << 20
        ),
    )(words, start, cols, grads)


def per_device(ex_n, par_n, gradients, inverse_gram, hash_words):
    amount = gradients.shape[1]
    feat_par, feat_ex = inverse_gram.shape
    piece = feat_par // ex_n
    e, p = lax.axis_index("ex"), lax.axis_index("par")
    ids = jnp.arange(feat_ex, dtype=jnp.int32)
    cols = (ids // piece) * feat_par + e * piece + ids % piece
    everyone = lax.all_gather(gradients, "ex", axis=0, tiled=True)
    partial = project(hash_words, (p * amount)[None], cols[None, :], everyone)
    summed = lax.psum_scatter(partial, "par", scatter_dimension=1, tiled=True)
    mine = (summed * FEATURES ** (-0.5)).astype(jnp.bfloat16)
    feat_p = lax.all_gather(mine, "ex", axis=1, tiled=True)
    pairs = []
    for src_e in range(ex_n):
        for src_p in range(par_n):
            pairs.append((src_e * par_n + src_p, src_p * ex_n + src_e))
    moved = lax.ppermute(mine, ("ex", "par"), pairs)
    feat_e = lax.all_gather(moved, "par", axis=1, tiled=True)
    parts = jnp.dot(feat_p, inverse_gram, preferred_element_type=jnp.float32)
    conditioned = lax.psum_scatter(parts, "par", scatter_dimension=0, tiled=True)
    scores = lax.dot_general(
        conditioned.astype(jnp.bfloat16),
        feat_e,
        (((1,), (1,)), ((), ())),
        preferred_element_type=jnp.float32,
    )
    scores = lax.psum_scatter(scores, "ex", scatter_dimension=1, tiled=True)
    return scores * FEATURES ** (-0.5)


def solution(mesh):
    return jax.shard_map(
        functools.partial(per_device, mesh.shape["ex"], mesh.shape["par"]),
        mesh=mesh,
        in_specs=(P("ex", "par"), P("par", "ex"), P()),
        out_specs=P("par", "ex"),
        check_vma=False,
    )
```

```python
import functools

import jax
import jax.numpy as jnp
from jax import lax
from jax.experimental import pallas as pl
from jax.experimental.pallas import tpu as pltpu
from jax.sharding import PartitionSpec as P

FEATURES = 16384


def shifted(values, amount):
    return lax.shift_right_logical(values, jnp.full(values.shape, amount, jnp.int32))


def hash_kernel(tile, words_ref, start_ref, cols_ref, grads_ref, out_ref):
    step = pl.program_id(0)
    depth = grads_ref.shape[1]
    m0 = words_ref[0] | 1
    m2 = words_ref[2] | 1
    m3 = words_ref[3] | 1
    row_base = (start_ref[0] + step * depth) * FEATURES * m0 + words_ref[1]
    rows = lax.broadcasted_iota(jnp.int32, (depth, tile), 0) * (m0 * FEATURES)
    grads = grads_ref[...]
    for first in range(0, out_ref.shape[1], tile):
        mixed = rows + (cols_ref[:, first:first + tile] * m0 + row_base)
        mixed = (mixed ^ shifted(mixed, 15)) * m2
        mixed = (mixed ^ shifted(mixed, 13)) * m3
        signs = jnp.where(mixed < 0, -1.0, 1.0).astype(jnp.bfloat16)
        part = jnp.dot(grads, signs, preferred_element_type=jnp.float32)

        @pl.when(step == 0)
        def _():
            out_ref[:, first:first + tile] = part

        @pl.when(step > 0)
        def _():
            out_ref[:, first:first + tile] += part


def project(words, start, cols, grads):
    rows, amount = grads.shape
    width = cols.shape[1]
    depth = min(512, amount)
    tile = min(512, width)
    return pl.pallas_call(
        functools.partial(hash_kernel, tile),
        grid=(amount // depth,),
        in_specs=[
            pl.BlockSpec(memory_space=pltpu.SMEM),
            pl.BlockSpec(memory_space=pltpu.SMEM),
            pl.BlockSpec((1, width), lambda k: (0, 0)),
            pl.BlockSpec((rows, depth), lambda k: (0, k)),
        ],
        out_specs=pl.BlockSpec((rows, width), lambda k: (0, 0)),
        out_shape=jax.ShapeDtypeStruct((rows, width), jnp.float32),
        compiler_params=pltpu.CompilerParams(
            dimension_semantics=("arbitrary",), vmem_limit_bytes=48 << 20
        ),
    )(words, start, cols, grads)


MESH = pl.DeviceIdType.MESH


def gather_kernel(ex_n, own_ref, out_ref, keep_sem, up_sem, down_sem, side_sem, recv_sem):
    e = lax.axis_index("ex")
    line, side = e // 2, e % 2
    last = ex_n // 2 - 1
    above, below, beside = lax.rem(e + 2, ex_n), lax.rem(e + ex_n - 2, ex_n), line * 2 + 1 - side
    barrier = pltpu.get_barrier_semaphore()

    def greet(peer):
        pl.semaphore_signal(barrier, inc=1, device_id={"ex": peer}, device_id_type=MESH)

    greet(beside)
    pl.when(line < last)(lambda: greet(above))
    pl.when(line > 0)(lambda: greet(below))
    inside = (line > 0) & (line < last)
    pl.when(inside)(lambda: pl.semaphore_wait(barrier, 3))
    pl.when(jnp.logical_not(inside))(lambda: pl.semaphore_wait(barrier, 2))

    def copy(src, slot, sems, peer):
        return pltpu.make_async_remote_copy(
            src_ref=src,
            dst_ref=out_ref.at[slot],
            send_sem=sems.at[slot],
            recv_sem=recv_sem.at[slot],
            device_id={"ex": peer},
            device_id_type=MESH,
        )

    keep = pltpu.make_async_copy(own_ref, out_ref.at[e], keep_sem)
    keep.start()
    pl.when(line < last)(lambda: copy(own_ref, e, up_sem, above).start())
    pl.when(line > 0)(lambda: copy(own_ref, e, down_sem, below).start())
    copy(own_ref, e, side_sem, beside).start()
    for far in range(1, last + 1):
        low, high = e - 2 * far, e + 2 * far

        @pl.when(line >= far)
        def _():
            copy(out_ref.at[low], low, up_sem, above).wait_recv()
            pl.when(line < last)(lambda: copy(out_ref.at[low], low, up_sem, above).start())
            copy(out_ref.at[low], low, side_sem, beside).start()

        @pl.when(line + far <= last)
        def _():
            copy(out_ref.at[high], high, down_sem, below).wait_recv()
            pl.when(line > 0)(lambda: copy(out_ref.at[high], high, down_sem, below).start())
            copy(out_ref.at[high], high, side_sem, beside).start()

    for spot in range(last + 1):
        mine, other = 2 * spot + side, 2 * spot + 1 - side
        copy(out_ref.at[other], other, side_sem, beside).wait_recv()
        copy(out_ref.at[mine], mine, side_sem, beside).wait_send()

        @pl.when((line < last) & (line >= spot))
        def _():
            copy(out_ref.at[mine], mine, up_sem, above).wait_send()

        @pl.when((line > 0) & (line <= spot))
        def _():
            copy(out_ref.at[mine], mine, down_sem, below).wait_send()

    keep.wait()


def gather(ex_n, own, collective_id):
    return pl.pallas_call(
        functools.partial(gather_kernel, ex_n),
        in_specs=[pl.BlockSpec(memory_space=pltpu.VMEM)],
        out_specs=pl.BlockSpec(memory_space=pl.ANY),
        out_shape=jax.ShapeDtypeStruct((ex_n,) + own.shape, own.dtype),
        scratch_shapes=[pltpu.SemaphoreType.DMA]
        + [pltpu.SemaphoreType.DMA((ex_n,)) for _ in range(4)],
        compiler_params=pltpu.CompilerParams(
            collective_id=collective_id, has_side_effects=True, vmem_limit_bytes=8 << 20
        ),
    )(own)


def scatter_kernel(ex_n, scale, in_ref, out_ref, landed, send_sem, recv_sem):
    e = lax.axis_index("ex")
    rows = out_ref.shape[0]
    barrier = pltpu.get_barrier_semaphore()
    for far in range(1, ex_n):
        peer = lax.rem(e + far, ex_n)
        pl.semaphore_signal(barrier, inc=1, device_id={"ex": peer}, device_id_type=MESH)
    pl.semaphore_wait(barrier, ex_n - 1)
    copies = []
    for far in range(1, ex_n):
        peer = lax.rem(e + far, ex_n)
        copies.append(
            pltpu.make_async_remote_copy(
                src_ref=in_ref.at[pl.ds(pl.multiple_of(peer * rows, rows), rows)],
                dst_ref=landed.at[far],
                send_sem=send_sem.at[far],
                recv_sem=recv_sem.at[far],
                device_id={"ex": peer},
                device_id_type=MESH,
            )
        )
        copies[-1].start()
    total = in_ref[pl.ds(pl.multiple_of(e * rows, rows), rows), :]
    for far in range(1, ex_n):
        copies[far - 1].wait_recv()
        total += landed[far]
    out_ref[...] = total * scale
    for each in copies:
        each.wait_send()


def scatter(ex_n, scale, stacked, collective_id):
    rows, columns = stacked.shape[0] // ex_n, stacked.shape[1]
    return pl.pallas_call(
        functools.partial(scatter_kernel, ex_n, scale),
        in_specs=[pl.BlockSpec(memory_space=pltpu.VMEM)],
        out_specs=pl.BlockSpec(memory_space=pltpu.VMEM),
        out_shape=jax.ShapeDtypeStruct((rows, columns), jnp.float32),
        scratch_shapes=[
            pltpu.VMEM((ex_n, rows, columns), jnp.float32),
            pltpu.SemaphoreType.DMA((ex_n,)),
            pltpu.SemaphoreType.DMA((ex_n,)),
        ],
        compiler_params=pltpu.CompilerParams(
            collective_id=collective_id, has_side_effects=True, vmem_limit_bytes=16 << 20
        ),
    )(stacked)


def tiles_kernel(feat_ref, gram_ref, out_ref):
    part = jnp.dot(feat_ref[0], gram_ref[...], preferred_element_type=jnp.float32)

    @pl.when(pl.program_id(0) == 0)
    def _():
        out_ref[...] = part

    @pl.when(pl.program_id(0) > 0)
    def _():
        out_ref[...] += part


def precondition(blocks, gram):
    count, rows, piece = blocks.shape
    width = gram.shape[1]
    return pl.pallas_call(
        tiles_kernel,
        grid=(count,),
        in_specs=[
            pl.BlockSpec((1, rows, piece), lambda k: (k, 0, 0)),
            pl.BlockSpec((piece, width), lambda k: (k, 0)),
        ],
        out_specs=pl.BlockSpec((rows, width), lambda k: (0, 0)),
        out_shape=jax.ShapeDtypeStruct((rows, width), jnp.float32),
        compiler_params=pltpu.CompilerParams(
            dimension_semantics=("arbitrary",), vmem_limit_bytes=48 << 20
        ),
    )(blocks, gram)


def per_device(ex_n, par_n, gradients, inverse_gram, hash_words):
    amount = gradients.shape[1]
    feat_par, feat_ex = inverse_gram.shape
    piece = feat_par // ex_n
    e, p = lax.axis_index("ex"), lax.axis_index("par")
    ids = jnp.arange(feat_ex, dtype=jnp.int32)
    cols = (ids // piece) * feat_par + e * piece + ids % piece
    everyone = gather(ex_n, gradients, 1).reshape(-1, amount)
    partial = project(hash_words, (p * amount)[None], cols[None, :], everyone)
    summed = lax.psum_scatter(partial, "par", scatter_dimension=1, tiled=True)
    mine = (summed * FEATURES ** (-0.5)).astype(jnp.bfloat16)
    pairs = []
    for src_e in range(ex_n):
        for src_p in range(par_n):
            pairs.append((src_e * par_n + src_p, src_p * ex_n + src_e))
    moved = lax.ppermute(mine, ("ex", "par"), pairs)
    feat_e = lax.all_gather(moved, "par", axis=1, tiled=True)
    blocks = gather(ex_n, mine, 2)
    parts = precondition(blocks, inverse_gram)
    conditioned = lax.psum_scatter(parts, "par", scatter_dimension=0, tiled=True)
    turned = lax.dot_general(
        feat_e,
        conditioned.astype(jnp.bfloat16),
        (((1,), (1,)), ((), ())),
        preferred_element_type=jnp.float32,
    )
    return scatter(ex_n, FEATURES ** (-0.5), turned, 3).T


def solution(mesh):
    return jax.shard_map(
        functools.partial(per_device, mesh.shape["ex"], mesh.shape["par"]),
        mesh=mesh,
        in_specs=(P("ex", "par"), P("par", "ex"), P()),
        out_specs=P("par", "ex"),
        check_vma=False,
    )
```

```python
import functools

import jax
import jax.numpy as jnp
from jax import lax
from jax.experimental import pallas as pl
from jax.experimental.pallas import tpu as pltpu
from jax.sharding import PartitionSpec as P

FEATURES = 16384


def shifted(values, amount):
    return lax.shift_right_logical(values, jnp.full(values.shape, amount, jnp.int32))


def hash_kernel(tile, words_ref, start_ref, cols_ref, grads_ref, out_ref):
    step = pl.program_id(0)
    depth = grads_ref.shape[1]
    m0 = words_ref[0] | 1
    m2 = words_ref[2] | 1
    m3 = words_ref[3] | 1
    row_base = (start_ref[0] + step * depth) * FEATURES * m0 + words_ref[1]
    rows = lax.broadcasted_iota(jnp.int32, (depth, tile), 0) * (m0 * FEATURES)
    grads = grads_ref[...]
    for spot in range(out_ref.shape[0]):
        first = spot * tile
        mixed = rows + (cols_ref[:, first:first + tile] * m0 + row_base)
        mixed = (mixed ^ shifted(mixed, 15)) * m2
        mixed = (mixed ^ shifted(mixed, 13)) * m3
        signs = jnp.where(mixed < 0, -1.0, 1.0).astype(jnp.bfloat16)
        part = jnp.dot(grads, signs, preferred_element_type=jnp.float32)

        @pl.when(step == 0)
        def _():
            out_ref[spot] = part

        @pl.when(step > 0)
        def _():
            out_ref[spot] += part


def project(words, start, cols, grads, tile):
    rows, amount = grads.shape
    width = cols.shape[1]
    depth = min(512, amount)
    return pl.pallas_call(
        functools.partial(hash_kernel, tile),
        grid=(amount // depth,),
        in_specs=[
            pl.BlockSpec(memory_space=pltpu.SMEM),
            pl.BlockSpec(memory_space=pltpu.SMEM),
            pl.BlockSpec((1, width), lambda k: (0, 0)),
            pl.BlockSpec((rows, depth), lambda k: (0, k)),
        ],
        out_specs=pl.BlockSpec((width // tile, rows, tile), lambda k: (0, 0, 0)),
        out_shape=jax.ShapeDtypeStruct((width // tile, rows, tile), jnp.float32),
        compiler_params=pltpu.CompilerParams(
            dimension_semantics=("arbitrary",), vmem_limit_bytes=48 << 20
        ),
    )(words, start, cols, grads)


MESH = pl.DeviceIdType.MESH


def gather_kernel(ex_n, own_ref, out_ref, keep_sem, up_sem, down_sem, side_sem, recv_sem):
    e = lax.axis_index("ex")
    line, side = e // 2, e % 2
    last = ex_n // 2 - 1
    above, below, beside = lax.rem(e + 2, ex_n), lax.rem(e + ex_n - 2, ex_n), line * 2 + 1 - side
    barrier = pltpu.get_barrier_semaphore()

    def greet(peer):
        pl.semaphore_signal(barrier, inc=1, device_id={"ex": peer}, device_id_type=MESH)

    greet(beside)
    pl.when(line < last)(lambda: greet(above))
    pl.when(line > 0)(lambda: greet(below))
    inside = (line > 0) & (line < last)
    pl.when(inside)(lambda: pl.semaphore_wait(barrier, 3))
    pl.when(jnp.logical_not(inside))(lambda: pl.semaphore_wait(barrier, 2))

    def copy(src, slot, sems, peer):
        return pltpu.make_async_remote_copy(
            src_ref=src,
            dst_ref=out_ref.at[slot],
            send_sem=sems.at[slot],
            recv_sem=recv_sem.at[slot],
            device_id={"ex": peer},
            device_id_type=MESH,
        )

    keep = pltpu.make_async_copy(own_ref, out_ref.at[e], keep_sem)
    keep.start()
    pl.when(line < last)(lambda: copy(own_ref, e, up_sem, above).start())
    pl.when(line > 0)(lambda: copy(own_ref, e, down_sem, below).start())
    copy(own_ref, e, side_sem, beside).start()
    for far in range(1, last + 1):
        low, high = e - 2 * far, e + 2 * far

        @pl.when(line >= far)
        def _():
            copy(out_ref.at[low], low, up_sem, above).wait_recv()
            pl.when(line < last)(lambda: copy(out_ref.at[low], low, up_sem, above).start())
            copy(out_ref.at[low], low, side_sem, beside).start()

        @pl.when(line + far <= last)
        def _():
            copy(out_ref.at[high], high, down_sem, below).wait_recv()
            pl.when(line > 0)(lambda: copy(out_ref.at[high], high, down_sem, below).start())
            copy(out_ref.at[high], high, side_sem, beside).start()

    for spot in range(last + 1):
        mine, other = 2 * spot + side, 2 * spot + 1 - side
        copy(out_ref.at[other], other, side_sem, beside).wait_recv()
        copy(out_ref.at[mine], mine, side_sem, beside).wait_send()

        @pl.when((line < last) & (line >= spot))
        def _():
            copy(out_ref.at[mine], mine, up_sem, above).wait_send()

        @pl.when((line > 0) & (line <= spot))
        def _():
            copy(out_ref.at[mine], mine, down_sem, below).wait_send()

    keep.wait()


def gather(ex_n, own, collective_id):
    return pl.pallas_call(
        functools.partial(gather_kernel, ex_n),
        in_specs=[pl.BlockSpec(memory_space=pltpu.VMEM)],
        out_specs=pl.BlockSpec(memory_space=pl.ANY),
        out_shape=jax.ShapeDtypeStruct((ex_n,) + own.shape, own.dtype),
        scratch_shapes=[pltpu.SemaphoreType.DMA]
        + [pltpu.SemaphoreType.DMA((ex_n,)) for _ in range(4)],
        compiler_params=pltpu.CompilerParams(
            collective_id=collective_id, has_side_effects=True, vmem_limit_bytes=8 << 20
        ),
    )(own)


def scatter_kernel(ex_n, scale, in_ref, out_ref, landed, send_sem, recv_sem):
    e = lax.axis_index("ex")
    rows = out_ref.shape[0]
    barrier = pltpu.get_barrier_semaphore()
    for far in range(1, ex_n):
        peer = lax.rem(e + far, ex_n)
        pl.semaphore_signal(barrier, inc=1, device_id={"ex": peer}, device_id_type=MESH)
    pl.semaphore_wait(barrier, ex_n - 1)
    copies = []
    for far in range(1, ex_n):
        peer = lax.rem(e + far, ex_n)
        copies.append(
            pltpu.make_async_remote_copy(
                src_ref=in_ref.at[pl.ds(pl.multiple_of(peer * rows, rows), rows)],
                dst_ref=landed.at[far],
                send_sem=send_sem.at[far],
                recv_sem=recv_sem.at[far],
                device_id={"ex": peer},
                device_id_type=MESH,
            )
        )
        copies[-1].start()
    total = in_ref[pl.ds(pl.multiple_of(e * rows, rows), rows), :]
    for far in range(1, ex_n):
        copies[far - 1].wait_recv()
        total += landed[far]
    out_ref[...] = total * scale
    for each in copies:
        each.wait_send()


def scatter(ex_n, scale, stacked, collective_id):
    rows, columns = stacked.shape[0] // ex_n, stacked.shape[1]
    return pl.pallas_call(
        functools.partial(scatter_kernel, ex_n, scale),
        in_specs=[pl.BlockSpec(memory_space=pltpu.VMEM)],
        out_specs=pl.BlockSpec(memory_space=pltpu.VMEM),
        out_shape=jax.ShapeDtypeStruct((rows, columns), jnp.float32),
        scratch_shapes=[
            pltpu.VMEM((ex_n, rows, columns), jnp.float32),
            pltpu.SemaphoreType.DMA((ex_n,)),
            pltpu.SemaphoreType.DMA((ex_n,)),
        ],
        compiler_params=pltpu.CompilerParams(
            collective_id=collective_id, has_side_effects=True, vmem_limit_bytes=16 << 20
        ),
    )(stacked)


def fold_kernel(chips, cuts, scale, in_ref, out_ref, near, staged, landed, near_send, near_recv, far_send, far_recv):
    p = lax.axis_index("par")
    x, core = p // 2, p % 2
    rows = in_ref.shape[1] // cuts
    partner = x * 2 + 1 - core
    barrier = pltpu.get_barrier_semaphore()
    pl.semaphore_signal(barrier, inc=1, device_id={"par": partner}, device_id_type=MESH)
    for d in range(1, chips):
        peer = lax.rem(x + d, chips) * 2 + core
        pl.semaphore_signal(barrier, inc=1, device_id={"par": peer}, device_id_type=MESH)
    pl.semaphore_wait(barrier, chips)
    order = [(d, c) for d in list(range(1, chips)) + [0] for c in range(cuts)]
    across, onward = {}, {}
    for d, c in order:
        part = pl.ds(c * rows, rows)
        across[d, c] = pltpu.make_async_remote_copy(
            src_ref=in_ref.at[lax.rem(x + d, chips) * 2 + 1 - core, part],
            dst_ref=near.at[d, part],
            send_sem=near_send.at[d, c],
            recv_sem=near_recv.at[d, c],
            device_id={"par": partner},
            device_id_type=MESH,
        )
        across[d, c].start()
    for d, c in order:
        part = pl.ds(c * rows, rows)
        across[d, c].wait_recv()
        total = in_ref[lax.rem(x + d, chips) * 2 + core, part, :] + near[d, part, :]
        staged[d, part, :] = total
        if d > 0:
            onward[d, c] = pltpu.make_async_remote_copy(
                src_ref=staged.at[d, part],
                dst_ref=landed.at[d, part],
                send_sem=far_send.at[d, c],
                recv_sem=far_recv.at[d, c],
                device_id={"par": lax.rem(x + d, chips) * 2 + core},
                device_id_type=MESH,
            )
            onward[d, c].start()
    for c in range(cuts):
        part = pl.ds(c * rows, rows)
        total = staged[0, part, :]
        for d in range(1, chips):
            onward[d, c].wait_recv()
            total += landed[d, part, :]
        out_ref[part, :] = (total * scale).astype(out_ref.dtype)
    for each in list(across.values()) + list(onward.values()):
        each.wait_send()


def fold(scale, stacked, collective_id):
    par_n, rows, columns = stacked.shape
    chips, cuts = par_n // 2, 4
    hold = pltpu.VMEM((chips, rows, columns), jnp.float32)
    return pl.pallas_call(
        functools.partial(fold_kernel, chips, cuts, scale),
        in_specs=[pl.BlockSpec(memory_space=pltpu.VMEM)],
        out_specs=pl.BlockSpec(memory_space=pltpu.VMEM),
        out_shape=jax.ShapeDtypeStruct((rows, columns), jnp.bfloat16),
        scratch_shapes=[hold, hold, hold]
        + [pltpu.SemaphoreType.DMA((chips, cuts)) for _ in range(4)],
        compiler_params=pltpu.CompilerParams(
            collective_id=collective_id, has_side_effects=True, vmem_limit_bytes=48 << 20
        ),
    )(stacked)


def tiles_kernel(feat_ref, gram_ref, out_ref):
    part = jnp.dot(feat_ref[0], gram_ref[...], preferred_element_type=jnp.float32)

    @pl.when(pl.program_id(0) == 0)
    def _():
        out_ref[...] = part

    @pl.when(pl.program_id(0) > 0)
    def _():
        out_ref[...] += part


def precondition(blocks, gram):
    count, rows, piece = blocks.shape
    width = gram.shape[1]
    return pl.pallas_call(
        tiles_kernel,
        grid=(count,),
        in_specs=[
            pl.BlockSpec((1, rows, piece), lambda k: (k, 0, 0)),
            pl.BlockSpec((piece, width), lambda k: (k, 0)),
        ],
        out_specs=pl.BlockSpec((rows, width), lambda k: (0, 0)),
        out_shape=jax.ShapeDtypeStruct((rows, width), jnp.float32),
        compiler_params=pltpu.CompilerParams(
            dimension_semantics=("arbitrary",), vmem_limit_bytes=48 << 20
        ),
        cost_estimate=pl.CostEstimate(
            flops=2 * count * rows * piece * width,
            bytes_accessed=2 * count * piece * (rows + width) + 4 * rows * width,
            transcendentals=0,
        ),
    )(blocks, gram)


def per_device(ex_n, par_n, gradients, inverse_gram, hash_words):
    amount = gradients.shape[1]
    feat_par, feat_ex = inverse_gram.shape
    piece = feat_par // ex_n
    e, p = lax.axis_index("ex"), lax.axis_index("par")
    ids = jnp.arange(feat_ex, dtype=jnp.int32)
    cols = (ids // piece) * feat_par + e * piece + ids % piece
    everyone = gather(ex_n, gradients, 1).reshape(-1, amount)
    partial = project(hash_words, (p * amount)[None], cols[None, :], everyone, piece)
    mine = fold(FEATURES ** (-0.5), partial, 4)
    blocks = gather(ex_n, mine, 2)
    mine, blocks = lax.optimization_barrier((mine, blocks))
    pairs = []
    for src_e in range(ex_n):
        for src_p in range(par_n):
            pairs.append((src_e * par_n + src_p, src_p * ex_n + src_e))
    moved = lax.ppermute(mine, ("ex", "par"), pairs)
    feat_e = lax.all_gather(moved, "par", axis=1, tiled=True)
    parts = precondition(blocks, inverse_gram)
    conditioned = fold(1.0, parts.reshape(par_n, -1, feat_ex), 5)
    turned = lax.dot_general(
        feat_e,
        conditioned,
        (((1,), (1,)), ((), ())),
        preferred_element_type=jnp.float32,
    )
    return scatter(ex_n, FEATURES ** (-0.5), turned, 3).T


def solution(mesh):
    return jax.shard_map(
        functools.partial(per_device, mesh.shape["ex"], mesh.shape["par"]),
        mesh=mesh,
        in_specs=(P("ex", "par"), P("par", "ex"), P()),
        out_specs=P("par", "ex"),
        check_vma=False,
    )
```

```python
import functools

import jax
import jax.numpy as jnp
from jax import lax
from jax.experimental import pallas as pl
from jax.experimental.pallas import tpu as pltpu
from jax.sharding import PartitionSpec as P

FEATURES = 16384


def shifted(values, amount):
    return lax.shift_right_logical(values, jnp.full(values.shape, amount, jnp.int32))


def hash_kernel(tile, words_ref, start_ref, cols_ref, grads_ref, out_ref):
    step = pl.program_id(0)
    depth = grads_ref.shape[1]
    m0 = words_ref[0] | 1
    m2 = words_ref[2] | 1
    m3 = words_ref[3] | 1
    row_base = (start_ref[0] + step * depth) * FEATURES * m0 + words_ref[1]
    rows = lax.broadcasted_iota(jnp.int32, (depth, tile), 0) * (m0 * FEATURES)
    grads = grads_ref[...]
    for spot in range(out_ref.shape[0]):
        first = spot * tile
        mixed = rows + (cols_ref[:, first:first + tile] * m0 + row_base)
        mixed = (mixed ^ shifted(mixed, 15)) * m2
        mixed = (mixed ^ shifted(mixed, 13)) * m3
        signs = jnp.where(mixed < 0, -1.0, 1.0).astype(jnp.bfloat16)
        part = jnp.dot(grads, signs, preferred_element_type=jnp.float32)

        @pl.when(step == 0)
        def _():
            out_ref[spot] = part

        @pl.when(step > 0)
        def _():
            out_ref[spot] += part


def project(words, start, cols, grads, tile):
    rows, amount = grads.shape
    width = cols.shape[1]
    depth = min(512, amount)
    return pl.pallas_call(
        functools.partial(hash_kernel, tile),
        grid=(amount // depth,),
        in_specs=[
            pl.BlockSpec(memory_space=pltpu.SMEM),
            pl.BlockSpec(memory_space=pltpu.SMEM),
            pl.BlockSpec((1, width), lambda k: (0, 0)),
            pl.BlockSpec((rows, depth), lambda k: (0, k)),
        ],
        out_specs=pl.BlockSpec((width // tile, rows, tile), lambda k: (0, 0, 0)),
        out_shape=jax.ShapeDtypeStruct((width // tile, rows, tile), jnp.float32),
        compiler_params=pltpu.CompilerParams(
            dimension_semantics=("arbitrary",), vmem_limit_bytes=48 << 20
        ),
    )(words, start, cols, grads)


MESH = pl.DeviceIdType.MESH


def gather_kernel(ex_n, own_ref, out_ref, keep_sem, up_sem, down_sem, side_sem, recv_sem):
    e = lax.axis_index("ex")
    line, side = e // 2, e % 2
    last = ex_n // 2 - 1
    above, below, beside = lax.rem(e + 2, ex_n), lax.rem(e + ex_n - 2, ex_n), line * 2 + 1 - side
    barrier = pltpu.get_barrier_semaphore()

    def greet(peer):
        pl.semaphore_signal(barrier, inc=1, device_id={"ex": peer}, device_id_type=MESH)

    greet(beside)
    pl.when(line < last)(lambda: greet(above))
    pl.when(line > 0)(lambda: greet(below))
    inside = (line > 0) & (line < last)
    pl.when(inside)(lambda: pl.semaphore_wait(barrier, 3))
    pl.when(jnp.logical_not(inside))(lambda: pl.semaphore_wait(barrier, 2))

    def copy(src, slot, sems, peer):
        return pltpu.make_async_remote_copy(
            src_ref=src,
            dst_ref=out_ref.at[slot],
            send_sem=sems.at[slot],
            recv_sem=recv_sem.at[slot],
            device_id={"ex": peer},
            device_id_type=MESH,
        )

    keep = pltpu.make_async_copy(own_ref, out_ref.at[e], keep_sem)
    keep.start()
    pl.when(line < last)(lambda: copy(own_ref, e, up_sem, above).start())
    pl.when(line > 0)(lambda: copy(own_ref, e, down_sem, below).start())
    copy(own_ref, e, side_sem, beside).start()
    for far in range(1, last + 1):
        low, high = e - 2 * far, e + 2 * far

        @pl.when(line >= far)
        def _():
            copy(out_ref.at[low], low, up_sem, above).wait_recv()
            pl.when(line < last)(lambda: copy(out_ref.at[low], low, up_sem, above).start())
            copy(out_ref.at[low], low, side_sem, beside).start()

        @pl.when(line + far <= last)
        def _():
            copy(out_ref.at[high], high, down_sem, below).wait_recv()
            pl.when(line > 0)(lambda: copy(out_ref.at[high], high, down_sem, below).start())
            copy(out_ref.at[high], high, side_sem, beside).start()

    for spot in range(last + 1):
        mine, other = 2 * spot + side, 2 * spot + 1 - side
        copy(out_ref.at[other], other, side_sem, beside).wait_recv()
        copy(out_ref.at[mine], mine, side_sem, beside).wait_send()

        @pl.when((line < last) & (line >= spot))
        def _():
            copy(out_ref.at[mine], mine, up_sem, above).wait_send()

        @pl.when((line > 0) & (line <= spot))
        def _():
            copy(out_ref.at[mine], mine, down_sem, below).wait_send()

    keep.wait()


def gather(ex_n, own, collective_id):
    return pl.pallas_call(
        functools.partial(gather_kernel, ex_n),
        in_specs=[pl.BlockSpec(memory_space=pltpu.VMEM)],
        out_specs=pl.BlockSpec(memory_space=pl.ANY),
        out_shape=jax.ShapeDtypeStruct((ex_n,) + own.shape, own.dtype),
        scratch_shapes=[pltpu.SemaphoreType.DMA]
        + [pltpu.SemaphoreType.DMA((ex_n,)) for _ in range(4)],
        compiler_params=pltpu.CompilerParams(
            collective_id=collective_id, has_side_effects=True, vmem_limit_bytes=8 << 20
        ),
    )(own)


def scatter_kernel(ex_n, scale, in_ref, out_ref, landed, send_sem, recv_sem):
    e = lax.axis_index("ex")
    rows = out_ref.shape[0]
    barrier = pltpu.get_barrier_semaphore()
    for far in range(1, ex_n):
        peer = lax.rem(e + far, ex_n)
        pl.semaphore_signal(barrier, inc=1, device_id={"ex": peer}, device_id_type=MESH)
    pl.semaphore_wait(barrier, ex_n - 1)
    copies = []
    for far in range(1, ex_n):
        peer = lax.rem(e + far, ex_n)
        copies.append(
            pltpu.make_async_remote_copy(
                src_ref=in_ref.at[pl.ds(pl.multiple_of(peer * rows, rows), rows)],
                dst_ref=landed.at[far],
                send_sem=send_sem.at[far],
                recv_sem=recv_sem.at[far],
                device_id={"ex": peer},
                device_id_type=MESH,
            )
        )
        copies[-1].start()
    total = in_ref[pl.ds(pl.multiple_of(e * rows, rows), rows), :]
    for far in range(1, ex_n):
        copies[far - 1].wait_recv()
        total += landed[far]
    out_ref[...] = total * scale
    for each in copies:
        each.wait_send()


def scatter(ex_n, scale, stacked, collective_id):
    rows, columns = stacked.shape[0] // ex_n, stacked.shape[1]
    return pl.pallas_call(
        functools.partial(scatter_kernel, ex_n, scale),
        in_specs=[pl.BlockSpec(memory_space=pltpu.VMEM)],
        out_specs=pl.BlockSpec(memory_space=pltpu.VMEM),
        out_shape=jax.ShapeDtypeStruct((rows, columns), jnp.float32),
        scratch_shapes=[
            pltpu.VMEM((ex_n, rows, columns), jnp.float32),
            pltpu.SemaphoreType.DMA((ex_n,)),
            pltpu.SemaphoreType.DMA((ex_n,)),
        ],
        compiler_params=pltpu.CompilerParams(
            collective_id=collective_id, has_side_effects=True, vmem_limit_bytes=16 << 20
        ),
    )(stacked)


def fold_kernel(chips, cuts, scale, in_ref, out_ref, near, staged, landed, near_send, near_recv, far_send, far_recv):
    p = lax.axis_index("par")
    x, core = p // 2, p % 2
    rows = in_ref.shape[1] // cuts
    partner = x * 2 + 1 - core
    barrier = pltpu.get_barrier_semaphore()
    pl.semaphore_signal(barrier, inc=1, device_id={"par": partner}, device_id_type=MESH)
    for d in range(1, chips):
        peer = lax.rem(x + d, chips) * 2 + core
        pl.semaphore_signal(barrier, inc=1, device_id={"par": peer}, device_id_type=MESH)
    pl.semaphore_wait(barrier, chips)
    order = [(d, c) for d in list(range(1, chips)) + [0] for c in range(cuts)]
    across, onward = {}, {}
    for d, c in order:
        part = pl.ds(c * rows, rows)
        across[d, c] = pltpu.make_async_remote_copy(
            src_ref=in_ref.at[lax.rem(x + d, chips) * 2 + 1 - core, part],
            dst_ref=near.at[d, part],
            send_sem=near_send.at[d, c],
            recv_sem=near_recv.at[d, c],
            device_id={"par": partner},
            device_id_type=MESH,
        )
        across[d, c].start()
    for d, c in order:
        part = pl.ds(c * rows, rows)
        across[d, c].wait_recv()
        total = in_ref[lax.rem(x + d, chips) * 2 + core, part, :] + near[d, part, :]
        staged[d, part, :] = total
        if d > 0:
            onward[d, c] = pltpu.make_async_remote_copy(
                src_ref=staged.at[d, part],
                dst_ref=landed.at[d, part],
                send_sem=far_send.at[d, c],
                recv_sem=far_recv.at[d, c],
                device_id={"par": lax.rem(x + d, chips) * 2 + core},
                device_id_type=MESH,
            )
            onward[d, c].start()
    for c in range(cuts):
        part = pl.ds(c * rows, rows)
        total = staged[0, part, :]
        for d in range(1, chips):
            onward[d, c].wait_recv()
            total += landed[d, part, :]
        out_ref[part, :] = (total * scale).astype(out_ref.dtype)
    for each in list(across.values()) + list(onward.values()):
        each.wait_send()


def fold(scale, stacked, dtype, collective_id):
    par_n, rows, columns = stacked.shape
    chips, cuts = par_n // 2, 4
    hold = pltpu.VMEM((chips, rows, columns), jnp.float32)
    return pl.pallas_call(
        functools.partial(fold_kernel, chips, cuts, scale),
        in_specs=[pl.BlockSpec(memory_space=pltpu.VMEM)],
        out_specs=pl.BlockSpec(memory_space=pltpu.VMEM),
        out_shape=jax.ShapeDtypeStruct((rows, columns), dtype),
        scratch_shapes=[hold, hold, hold]
        + [pltpu.SemaphoreType.DMA((chips, cuts)) for _ in range(4)],
        compiler_params=pltpu.CompilerParams(
            collective_id=collective_id, has_side_effects=True, vmem_limit_bytes=48 << 20
        ),
    )(stacked)


def tiles_kernel(feat_ref, gram_ref, out_ref):
    step = pl.program_id(0)
    tile = out_ref.shape[2]
    for spot in range(out_ref.shape[0]):
        gram = gram_ref[:, spot * tile:(spot + 1) * tile]
        part = jnp.dot(feat_ref[0], gram, preferred_element_type=jnp.float32)

        @pl.when(step == 0)
        def _():
            out_ref[spot] = part

        @pl.when(step > 0)
        def _():
            out_ref[spot] += part


def precondition(blocks, gram, tile):
    count, rows, piece = blocks.shape
    width = gram.shape[1]
    return pl.pallas_call(
        tiles_kernel,
        grid=(count,),
        in_specs=[
            pl.BlockSpec((1, rows, piece), lambda k: (k, 0, 0)),
            pl.BlockSpec((piece, width), lambda k: (k, 0)),
        ],
        out_specs=pl.BlockSpec((width // tile, rows, tile), lambda k: (0, 0, 0)),
        out_shape=jax.ShapeDtypeStruct((width // tile, rows, tile), jnp.float32),
        compiler_params=pltpu.CompilerParams(
            dimension_semantics=("arbitrary",), vmem_limit_bytes=48 << 20
        ),
        cost_estimate=pl.CostEstimate(
            flops=2 * count * rows * piece * width,
            bytes_accessed=2 * count * piece * (rows + width) + 4 * rows * width,
            transcendentals=0,
        ),
    )(blocks, gram)


def per_device(ex_n, par_n, gradients, inverse_gram, hash_words):
    amount = gradients.shape[1]
    feat_par, feat_ex = inverse_gram.shape
    piece = feat_par // ex_n
    e, p = lax.axis_index("ex"), lax.axis_index("par")
    ids = jnp.arange(feat_ex, dtype=jnp.int32)
    cols = (ids // piece) * feat_par + e * piece + ids % piece
    everyone = gather(ex_n, gradients, 1).reshape(-1, amount)
    partial = project(hash_words, (p * amount)[None], cols[None, :], everyone, piece)
    mine = fold(FEATURES ** (-0.5), partial, jnp.bfloat16, 4)
    blocks = gather(ex_n, mine, 2)
    mine, blocks = lax.optimization_barrier((mine, blocks))
    pairs = []
    for src_e in range(ex_n):
        for src_p in range(par_n):
            pairs.append((src_e * par_n + src_p, src_p * ex_n + src_e))
    moved = lax.ppermute(mine, ("ex", "par"), pairs)
    parts = precondition(blocks, inverse_gram, piece)
    conditioned = fold(1.0, parts, jnp.bfloat16, 5)
    pairs = lax.dot_general(
        conditioned,
        moved,
        (((1,), (1,)), ((), ())),
        preferred_element_type=jnp.float32,
    )
    rows = fold(1.0, pairs.reshape(par_n, -1, pairs.shape[1]), jnp.float32, 6)
    return scatter(ex_n, FEATURES ** (-0.5), rows.T, 3).T


def solution(mesh):
    return jax.shard_map(
        functools.partial(per_device, mesh.shape["ex"], mesh.shape["par"]),
        mesh=mesh,
        in_specs=(P("ex", "par"), P("par", "ex"), P()),
        out_specs=P("par", "ex"),
        check_vma=False,
    )
```

```python
import functools

import jax
import jax.numpy as jnp
from jax import lax
from jax.experimental import pallas as pl
from jax.experimental.pallas import tpu as pltpu
from jax.sharding import PartitionSpec as P

FEATURES = 16384


def shifted(values, amount):
    return lax.shift_right_logical(values, jnp.full(values.shape, amount, jnp.int32))


def hash_kernel(tile, words_ref, start_ref, cols_ref, grads_ref, out_ref):
    step = pl.program_id(0)
    depth = grads_ref.shape[1]
    m0 = words_ref[0] | 1
    m2 = words_ref[2] | 1
    m3 = words_ref[3] | 1
    row_base = (start_ref[0] + step * depth) * FEATURES * m0 + words_ref[1]
    rows = lax.broadcasted_iota(jnp.int32, (depth, tile), 0) * (m0 * FEATURES)
    grads = grads_ref[...]
    for spot in range(out_ref.shape[0]):
        first = spot * tile
        mixed = rows + (cols_ref[:, first:first + tile] * m0 + row_base)
        mixed = (mixed ^ shifted(mixed, 15)) * m2
        mixed = (mixed ^ shifted(mixed, 13)) * m3
        signs = jnp.where(mixed < 0, -1.0, 1.0).astype(jnp.bfloat16)
        part = jnp.dot(grads, signs, preferred_element_type=jnp.float32)

        @pl.when(step == 0)
        def _():
            out_ref[spot] = part

        @pl.when(step > 0)
        def _():
            out_ref[spot] += part


def project(words, start, cols, grads, tile):
    rows, amount = grads.shape
    width = cols.shape[1]
    depth = min(512, amount)
    return pl.pallas_call(
        functools.partial(hash_kernel, tile),
        grid=(amount // depth,),
        in_specs=[
            pl.BlockSpec(memory_space=pltpu.SMEM),
            pl.BlockSpec(memory_space=pltpu.SMEM),
            pl.BlockSpec((1, width), lambda k: (0, 0)),
            pl.BlockSpec((rows, depth), lambda k: (0, k)),
        ],
        out_specs=pl.BlockSpec((width // tile, rows, tile), lambda k: (0, 0, 0)),
        out_shape=jax.ShapeDtypeStruct((width // tile, rows, tile), jnp.float32),
        compiler_params=pltpu.CompilerParams(
            dimension_semantics=("arbitrary",), vmem_limit_bytes=48 << 20
        ),
    )(words, start, cols, grads)


MESH = pl.DeviceIdType.MESH


def gather_kernel(ex_n, own_ref, out_ref, keep_sem, up_sem, down_sem, side_sem, recv_sem):
    e = lax.axis_index("ex")
    line, side = e // 2, e % 2
    last = ex_n // 2 - 1
    above, below, beside = lax.rem(e + 2, ex_n), lax.rem(e + ex_n - 2, ex_n), line * 2 + 1 - side
    barrier = pltpu.get_barrier_semaphore()

    def greet(peer):
        pl.semaphore_signal(barrier, inc=1, device_id={"ex": peer}, device_id_type=MESH)

    greet(beside)
    pl.when(line < last)(lambda: greet(above))
    pl.when(line > 0)(lambda: greet(below))
    inside = (line > 0) & (line < last)
    pl.when(inside)(lambda: pl.semaphore_wait(barrier, 3))
    pl.when(jnp.logical_not(inside))(lambda: pl.semaphore_wait(barrier, 2))

    def copy(src, slot, sems, peer):
        return pltpu.make_async_remote_copy(
            src_ref=src,
            dst_ref=out_ref.at[slot],
            send_sem=sems.at[slot],
            recv_sem=recv_sem.at[slot],
            device_id={"ex": peer},
            device_id_type=MESH,
        )

    keep = pltpu.make_async_copy(own_ref, out_ref.at[e], keep_sem)
    keep.start()
    pl.when(line < last)(lambda: copy(own_ref, e, up_sem, above).start())
    pl.when(line > 0)(lambda: copy(own_ref, e, down_sem, below).start())
    copy(own_ref, e, side_sem, beside).start()
    for far in range(1, last + 1):
        low, high = e - 2 * far, e + 2 * far

        @pl.when(line >= far)
        def _():
            copy(out_ref.at[low], low, up_sem, above).wait_recv()
            pl.when(line < last)(lambda: copy(out_ref.at[low], low, up_sem, above).start())
            copy(out_ref.at[low], low, side_sem, beside).start()

        @pl.when(line + far <= last)
        def _():
            copy(out_ref.at[high], high, down_sem, below).wait_recv()
            pl.when(line > 0)(lambda: copy(out_ref.at[high], high, down_sem, below).start())
            copy(out_ref.at[high], high, side_sem, beside).start()

    for spot in range(last + 1):
        mine, other = 2 * spot + side, 2 * spot + 1 - side
        copy(out_ref.at[other], other, side_sem, beside).wait_recv()
        copy(out_ref.at[mine], mine, side_sem, beside).wait_send()

        @pl.when((line < last) & (line >= spot))
        def _():
            copy(out_ref.at[mine], mine, up_sem, above).wait_send()

        @pl.when((line > 0) & (line <= spot))
        def _():
            copy(out_ref.at[mine], mine, down_sem, below).wait_send()

    keep.wait()


def gather(ex_n, own, collective_id):
    return pl.pallas_call(
        functools.partial(gather_kernel, ex_n),
        in_specs=[pl.BlockSpec(memory_space=pltpu.VMEM)],
        out_specs=pl.BlockSpec(memory_space=pl.ANY),
        out_shape=jax.ShapeDtypeStruct((ex_n,) + own.shape, own.dtype),
        scratch_shapes=[pltpu.SemaphoreType.DMA]
        + [pltpu.SemaphoreType.DMA((ex_n,)) for _ in range(4)],
        compiler_params=pltpu.CompilerParams(
            collective_id=collective_id, has_side_effects=True, vmem_limit_bytes=8 << 20
        ),
    )(own)


def scatter_kernel(ex_n, scale, in_ref, out_ref, landed, send_sem, recv_sem):
    e = lax.axis_index("ex")
    rows = out_ref.shape[0]
    barrier = pltpu.get_barrier_semaphore()
    for far in range(1, ex_n):
        peer = lax.rem(e + far, ex_n)
        pl.semaphore_signal(barrier, inc=1, device_id={"ex": peer}, device_id_type=MESH)
    pl.semaphore_wait(barrier, ex_n - 1)
    copies = []
    for far in range(1, ex_n):
        peer = lax.rem(e + far, ex_n)
        copies.append(
            pltpu.make_async_remote_copy(
                src_ref=in_ref.at[pl.ds(pl.multiple_of(peer * rows, rows), rows)],
                dst_ref=landed.at[far],
                send_sem=send_sem.at[far],
                recv_sem=recv_sem.at[far],
                device_id={"ex": peer},
                device_id_type=MESH,
            )
        )
        copies[-1].start()
    total = in_ref[pl.ds(pl.multiple_of(e * rows, rows), rows), :]
    for far in range(1, ex_n):
        copies[far - 1].wait_recv()
        total += landed[far]
    out_ref[...] = total * scale
    for each in copies:
        each.wait_send()


def scatter(ex_n, scale, stacked, collective_id):
    rows, columns = stacked.shape[0] // ex_n, stacked.shape[1]
    return pl.pallas_call(
        functools.partial(scatter_kernel, ex_n, scale),
        in_specs=[pl.BlockSpec(memory_space=pltpu.VMEM)],
        out_specs=pl.BlockSpec(memory_space=pltpu.VMEM),
        out_shape=jax.ShapeDtypeStruct((rows, columns), jnp.float32),
        scratch_shapes=[
            pltpu.VMEM((ex_n, rows, columns), jnp.float32),
            pltpu.SemaphoreType.DMA((ex_n,)),
            pltpu.SemaphoreType.DMA((ex_n,)),
        ],
        compiler_params=pltpu.CompilerParams(
            collective_id=collective_id, has_side_effects=True, vmem_limit_bytes=16 << 20
        ),
    )(stacked)


def fold_kernel(chips, cuts, scale, in_ref, out_ref, near, staged, landed, near_send, near_recv, far_send, far_recv):
    p = lax.axis_index("par")
    x, core = p // 2, p % 2
    rows = in_ref.shape[1] // cuts
    partner = x * 2 + 1 - core
    barrier = pltpu.get_barrier_semaphore()
    pl.semaphore_signal(barrier, inc=1, device_id={"par": partner}, device_id_type=MESH)
    for d in range(1, chips):
        peer = lax.rem(x + d, chips) * 2 + core
        pl.semaphore_signal(barrier, inc=1, device_id={"par": peer}, device_id_type=MESH)
    pl.semaphore_wait(barrier, chips)
    order = [(d, c) for d in list(range(1, chips)) + [0] for c in range(cuts)]
    across, onward = {}, {}
    for d, c in order:
        part = pl.ds(c * rows, rows)
        across[d, c] = pltpu.make_async_remote_copy(
            src_ref=in_ref.at[lax.rem(x + d, chips) * 2 + 1 - core, part],
            dst_ref=near.at[d, part],
            send_sem=near_send.at[d, c],
            recv_sem=near_recv.at[d, c],
            device_id={"par": partner},
            device_id_type=MESH,
        )
        across[d, c].start()
    for d, c in order:
        part = pl.ds(c * rows, rows)
        across[d, c].wait_recv()
        total = in_ref[lax.rem(x + d, chips) * 2 + core, part, :] + near[d, part, :]
        staged[d, part, :] = total
        if d > 0:
            onward[d, c] = pltpu.make_async_remote_copy(
                src_ref=staged.at[d, part],
                dst_ref=landed.at[d, part],
                send_sem=far_send.at[d, c],
                recv_sem=far_recv.at[d, c],
                device_id={"par": lax.rem(x + d, chips) * 2 + core},
                device_id_type=MESH,
            )
            onward[d, c].start()
    for c in range(cuts):
        part = pl.ds(c * rows, rows)
        total = staged[0, part, :]
        for d in range(1, chips):
            onward[d, c].wait_recv()
            total += landed[d, part, :]
        out_ref[part, :] = (total * scale).astype(out_ref.dtype)
    for each in list(across.values()) + list(onward.values()):
        each.wait_send()


def fold(scale, stacked, dtype, collective_id):
    par_n, rows, columns = stacked.shape
    chips = par_n // 2
    cuts = 8 if rows * columns >= 1 << 18 else 2
    hold = pltpu.VMEM((chips, rows, columns), jnp.float32)
    return pl.pallas_call(
        functools.partial(fold_kernel, chips, cuts, scale),
        in_specs=[pl.BlockSpec(memory_space=pltpu.VMEM)],
        out_specs=pl.BlockSpec(memory_space=pltpu.VMEM),
        out_shape=jax.ShapeDtypeStruct((rows, columns), dtype),
        scratch_shapes=[hold, hold, hold]
        + [pltpu.SemaphoreType.DMA((chips, cuts)) for _ in range(4)],
        compiler_params=pltpu.CompilerParams(
            collective_id=collective_id, has_side_effects=True, vmem_limit_bytes=48 << 20
        ),
    )(stacked)


def tiles_kernel(feat_ref, gram_ref, out_ref):
    step = pl.program_id(0)
    tile = out_ref.shape[2]
    for spot in range(out_ref.shape[0]):
        gram = gram_ref[:, spot * tile:(spot + 1) * tile]
        part = jnp.dot(feat_ref[0], gram, preferred_element_type=jnp.float32)

        @pl.when(step == 0)
        def _():
            out_ref[spot] = part

        @pl.when(step > 0)
        def _():
            out_ref[spot] += part


def precondition(blocks, gram, tile):
    count, rows, piece = blocks.shape
    width = gram.shape[1]
    return pl.pallas_call(
        tiles_kernel,
        grid=(count,),
        in_specs=[
            pl.BlockSpec((1, rows, piece), lambda k: (k, 0, 0)),
            pl.BlockSpec((piece, width), lambda k: (k, 0)),
        ],
        out_specs=pl.BlockSpec((width // tile, rows, tile), lambda k: (0, 0, 0)),
        out_shape=jax.ShapeDtypeStruct((width // tile, rows, tile), jnp.float32),
        compiler_params=pltpu.CompilerParams(
            dimension_semantics=("arbitrary",), vmem_limit_bytes=48 << 20
        ),
        cost_estimate=pl.CostEstimate(
            flops=2 * count * rows * piece * width,
            bytes_accessed=2 * count * piece * (rows + width) + 4 * rows * width,
            transcendentals=0,
        ),
    )(blocks, gram)


def per_device(ex_n, par_n, gradients, inverse_gram, hash_words):
    amount = gradients.shape[1]
    feat_par, feat_ex = inverse_gram.shape
    piece = feat_par // ex_n
    e, p = lax.axis_index("ex"), lax.axis_index("par")
    ids = jnp.arange(feat_ex, dtype=jnp.int32)
    cols = (ids // piece) * feat_par + e * piece + ids % piece
    everyone = gather(ex_n, gradients, 1).reshape(-1, amount)
    partial = project(hash_words, (p * amount)[None], cols[None, :], everyone, piece)
    mine = fold(FEATURES ** (-0.5), partial, jnp.bfloat16, 4)
    blocks = gather(ex_n, mine, 2)
    mine, blocks = lax.optimization_barrier((mine, blocks))
    pairs = []
    for src_e in range(ex_n):
        for src_p in range(par_n):
            pairs.append((src_e * par_n + src_p, src_p * ex_n + src_e))
    moved = lax.ppermute(mine, ("ex", "par"), pairs)
    parts = precondition(blocks, inverse_gram, piece)
    conditioned = fold(1.0, parts, jnp.bfloat16, 5)
    pairs = lax.dot_general(
        conditioned,
        moved,
        (((1,), (1,)), ((), ())),
        preferred_element_type=jnp.float32,
    )
    rows = fold(1.0, pairs.reshape(par_n, -1, pairs.shape[1]), jnp.float32, 6)
    return scatter(ex_n, FEATURES ** (-0.5), rows.T, 3).T


def solution(mesh):
    return jax.shard_map(
        functools.partial(per_device, mesh.shape["ex"], mesh.shape["par"]),
        mesh=mesh,
        in_specs=(P("ex", "par"), P("par", "ex"), P()),
        out_specs=P("par", "ex"),
        check_vma=False,
    )
```
